32 devices in a mesh: rep: 4 (over x, core), exp: 8 (over z, y).
Axes of the slice: x: 2, y: 2, z: 4, core: 2. Of those that a mesh axis runs over, the one named last changes fastest.
Arguments:
- inputs: bfloat16 [4096, 2048], P(('rep', 'exp')), may hold values from -6 to 6
- out_grad: bfloat16 [4096, 2048], P(('rep', 'exp')), may hold values from -6 to 6
- routes: int32 [4096, 8], P(('rep', 'exp')), may hold values from 0 to 63, all different within a row; in each aligned block of 128 rows (0 to 127, 128 to 255, ...) at most 18 rows name the same one
- gates: float32 [4096, 8], P(('rep', 'exp')), may hold values from 0.05 to 0.3
- weights: bfloat16 [2048, 64, 3, 384], P('rep', 'exp'), may hold values from -0.125 to 0.125
- moment_one: float32 [2048, 64, 3, 384], P('rep', 'exp'), may hold values from -18 to 18
- moment_two: float32 [2048, 64, 3, 384], P('rep', 'exp'), may hold values from 1 to 100
Outputs:
- input_grad: bfloat16 [4096, 2048], P(('rep', 'exp'))
- first_moment: float32 [2048, 64, 3, 384], P('rep', 'exp')
- second_moment: float32 [2048, 64, 3, 384], P('rep', 'exp')
- new_weights: bfloat16 [2048, 64, 3, 384], P('rep', 'exp')
The draws below stay inside these ranges and needn't reach their ends.
Inputs may be any that keep to these rules, and one draw needn't show every extreme that they name: `routes`: each row names 8 different experts. In the rows of one device no expert is named by more than 18 rows, a bound that some block reaches.
All inputs are finite; a program needn't handle non-finite values.
Results may differ from the reference program's by a relative error of at most 0.0064.
Values may be sent and summed in bfloat16 or wider, within the bound.
A program may use at most 384 MiB of HBM per device.

```python
import math
import jax
import jax.numpy as jnp
import numpy as np
from jax import lax

D = 2048
E = 64
FFN = 384
TOP = 8
TOK_DEV = 128
CAP = 18
TOKENS = 4096
N_REP = 4
N_EXP = 8


def shard_levels(stream_key, dims, shards, smallest, largest):
    gain = 1.0
    for dim, shards_of in shards:
        steps = jax.random.uniform(jax.random.fold_in(jax.random.fold_in(stream_key, 6), dim), (shards_of,), jnp.float32, smallest / len(shards), largest / len(shards))
        gain = gain * jnp.repeat(jnp.exp(steps), dims[dim] // shards_of).reshape((-1,) + (1,) * (len(dims) - 1 - dim))
    return gain


def deal_out(own_key, own, number, rows, number_of, top, bound, slope):
    ranking = jax.random.permutation(own_key, number_of)
    crowded, ordinary = shares(number_of, rows * top, bound, slope, True), shares(number_of, rows * top, bound, slope, False)
    places = jnp.arange(number_of)

    def named(lengths, turn):
        used = int((lengths > 0).sum())
        fixed = max(1, used // 4)
        shifted = fixed + (places - fixed + turn * (used - fixed)) % max(1, number_of - fixed)
        return jnp.zeros((number_of,), jnp.int32).at[ranking[jnp.where(places < fixed, places, shifted)]].set(jnp.asarray(lengths, jnp.int32))

    lengths = jnp.where(number % 4 == 0, named(crowded, number // 4), named(ordinary, number - number // 4 - 1))
    mixed = jax.random.permutation(jax.random.fold_in(own, 3), number_of)
    source_of, receiver = mixed[0:number_of // 2 * 2:2], mixed[1:number_of // 2 * 2:2]
    room = jnp.minimum(lengths[source_of] - 1, bound - lengths[receiver]) // 2
    room = jnp.where((source_of == ranking[0]) | (receiver == ranking[0]) | (lengths[receiver] == 0), 0, jnp.maximum(room, 0))
    shifted = jax.random.randint(jax.random.fold_in(own, 4), (number_of // 2,), 0, 1 << 20) % (room + 1)
    lengths = lengths.at[source_of].add(-shifted).at[receiver].add(shifted)
    members = jnp.searchsorted(jnp.cumsum(lengths), jnp.arange(rows * top), side="right").astype(jnp.int32)
    grid = members.reshape(top, rows).T
    grid = grid[jax.random.permutation(jax.random.fold_in(own, 1), rows)]
    turn = jax.random.randint(jax.random.fold_in(own, 2), (rows, 1), 0, top)
    return jnp.take_along_axis(grid, (jnp.arange(top)[None, :] + turn) % top, axis=1)


def shares(number_of, total, most, skew, full):
    loads = [(1 << 20) // math.isqrt(grade ** skew) + 1 for grade in range(1, number_of + 1)]
    largest = most if full else min(most, max(-(-total // number_of), total * loads[0] // sum(loads)))
    least = 1 if total - largest >= number_of - 1 else 0
    given, rest = [largest] + [least] * (number_of - 1), total - largest - least * (number_of - 1)
    while rest > 0:
        movable = [i for i in range(1, number_of) if given[i] < largest] or [i for i in range(1, number_of) if given[i] < most]
        pool, left = sum([loads[i] for i in movable]), rest
        for i in movable:
            addition = min(most - given[i], max(1, left * loads[i] // pool), rest)
            given[i] = given[i] + addition
            rest = rest - addition
    return np.array(given)


def bell_draw(rng, dims, width, most, pieces=(), kind=jnp.bfloat16):
    values = width * jax.random.normal(rng, dims, jnp.float32)
    if pieces:
        values = values * shard_levels(rng, dims, pieces, -0.22, 0.18)
    return jnp.clip(values, -most, most).astype(kind)


def setup_inputs(seed: int = 0) -> dict:
    arg_keys = jax.random.split(jax.random.key(seed), 8)
    inputs = bell_draw(arg_keys[0], (TOKENS, D), 1.0, 6.0, ((0, 32),))
    out_grad = bell_draw(arg_keys[1], (TOKENS, D), 1.0, 6.0, ((0, 32),))
    routes_keys = jax.random.split(jax.random.fold_in(arg_keys[2], 1), TOKENS // TOK_DEV)
    routes_turns = jax.random.permutation(jax.random.fold_in(arg_keys[2], 3), TOKENS // TOK_DEV)
    routes = jax.vmap(lambda own, number: deal_out(jax.random.fold_in(arg_keys[2], 2), own, number, TOK_DEV, E, TOP, CAP, 0))(routes_keys, routes_turns).reshape((TOKENS, TOP))
    gates = jnp.clip(0.05 + 0.25 * jax.random.uniform(arg_keys[3], (TOKENS, TOP), jnp.float32) ** shard_levels(arg_keys[3], (TOKENS, TOP), ((0, 32),), -0.2, 0.2), 0.05, 0.3)
    weights = bell_draw(arg_keys[4], (D, E, 3, FFN), D ** -0.5, 0.125, ((0, 4), (1, 8)))
    moment_one = bell_draw(arg_keys[5], (D, E, 3, FFN), 3.0, 18.0, ((0, 4), (1, 8)), jnp.float32)
    moment_two = jnp.clip(jnp.exp(math.log(100.0) - 4.6051702 * jax.random.uniform(arg_keys[6], (D, E, 3, FFN), jnp.float32) ** shard_levels(arg_keys[6], (D, E, 3, FFN), ((0, 4), (1, 8)), -0.2, 0.2)), 1.0, 100.0)
    return {"inputs": inputs, "out_grad": out_grad, "routes": routes, "gates": gates, "weights": weights, "moment_one": moment_one, "moment_two": moment_two}


beta_one = 0.9
beta_two = 0.95
learn_rate = 0.002
decay_rate = 0.1
epsilon = 1e-08
step_count = 100

def slot_positions(routes):
    blocks = routes.reshape(N_REP * N_EXP, TOK_DEV * TOP)
    expert_ids = jnp.arange(E, dtype=jnp.int32)

    def one_block(block):
        onehot = (block[:, None] == expert_ids[None, :]).astype(jnp.int32)
        before = jnp.cumsum(onehot, axis=0) - onehot
        slot = lax.optimization_barrier(jnp.sum(before * onehot, axis=1))
        return block * CAP + slot
    return jax.vmap(one_block)(blocks)

def reference(inputs, out_grad, routes, gates, weights, moment_one, moment_two):
    nblocks = N_REP * N_EXP
    position = slot_positions(routes)
    pair_ids = jnp.broadcast_to(jnp.arange(TOK_DEV * TOP, dtype=jnp.int32)[None, :], position.shape)
    block_ids = jnp.broadcast_to(jnp.arange(nblocks, dtype=jnp.int32)[:, None], position.shape)
    table = jnp.full((nblocks, E * CAP), -1, jnp.int32).at[block_ids, position].set(pair_ids)

    def per_expert(carry, expert):
        cols = lax.dynamic_slice_in_dim(table, (expert * CAP).astype(jnp.int32), CAP, 1)
        valid = cols >= 0
        safe = jnp.where(valid, cols, 0)
        token = (jnp.arange(nblocks, dtype=jnp.int32)[:, None] * TOK_DEV + safe // TOP).astype(jnp.int32)
        pair_k = (safe % TOP).astype(jnp.int32)
        rows_x = jnp.where(valid[..., None], inputs[token], jnp.zeros((), inputs.dtype)).reshape(-1, D)
        gate = gates[token, pair_k]
        scaled = (gate[..., None] * out_grad[token].astype(jnp.float32)).astype(jnp.bfloat16)
        rows_g = jnp.where(valid[..., None], scaled, jnp.zeros((), scaled.dtype)).reshape(-1, D)
        mats = weights[:, expert]
        w_gate = mats[:, 0]
        w_up = mats[:, 1]
        w_down = mats[:, 2]
        hg = jnp.dot(rows_x, w_gate, preferred_element_type=jnp.float32)
        hu = jnp.dot(rows_x, w_up, preferred_element_type=jnp.float32)
        sig = jax.nn.sigmoid(hg)
        act = (hg * sig * hu).astype(jnp.bfloat16)
        da = jnp.dot(rows_g, w_down, preferred_element_type=jnp.float32)
        dhu = (da * hg * sig).astype(jnp.bfloat16)
        dhg = (da * hu * sig * (1.0 + hg * (1.0 - sig))).astype(jnp.bfloat16)
        slot_dx = (jnp.dot(dhg, w_gate.T, preferred_element_type=jnp.float32) + jnp.dot(dhu, w_up.T, preferred_element_type=jnp.float32)).astype(jnp.bfloat16)
        g_gate = jnp.dot(rows_x.T, dhg, preferred_element_type=jnp.float32)
        g_up = jnp.dot(rows_x.T, dhu, preferred_element_type=jnp.float32)
        g_down = jnp.dot(rows_g.T, act, preferred_element_type=jnp.float32)
        carry = carry.at[token.reshape(-1)].add(slot_dx.astype(jnp.float32))
        return (carry, jnp.stack([g_gate, g_up, g_down], axis=1))
    start = jnp.zeros((N_REP * N_EXP * TOK_DEV, D), jnp.float32)
    dx_total, grads = lax.scan(per_expert, start, jnp.arange(E, dtype=jnp.int32))
    grad = jnp.transpose(grads, (1, 0, 2, 3))
    first_moment = beta_one * moment_one + (1.0 - beta_one) * grad
    second_moment = beta_two * moment_two + (1.0 - beta_two) * grad * grad
    correct_one = 1.0 - beta_one ** step_count
    correct_two = 1.0 - beta_two ** step_count
    weights32 = weights.astype(jnp.float32)
    update = first_moment / correct_one / (jnp.sqrt(second_moment / correct_two) + epsilon) + decay_rate * weights32
    new_weights = (weights32 - learn_rate * update).astype(jnp.bfloat16)
    return (dx_total.astype(jnp.bfloat16), first_moment, second_moment, new_weights)
```

```python
import jax
import jax.numpy as jnp
from jax import lax
from jax.experimental.layout import Layout, with_layout_constraint
from jax.sharding import PartitionSpec as P

CAP = 18


beta_one = 0.9
beta_two = 0.95
learn_rate = 0.002
decay_rate = 0.1
epsilon = 1e-08
step_count = 100

F32 = jnp.float32
BF16 = jnp.bfloat16


def per_device(inputs, out_grad, routes, gates, weights, moment_one, moment_two):
    replicas, sources = lax.axis_size("rep"), lax.axis_size("exp")
    tok_dev, top = routes.shape
    part, local, kinds, ffn = weights.shape
    group = replicas * tok_dev
    slots = replicas * CAP
    pair = 2 * ffn

    meta = jnp.stack([routes.astype(F32).T, gates.T])
    meta = lax.all_gather(meta, ("rep", "exp"), axis=0, tiled=False)
    meta = meta.reshape(replicas, sources, 2, top, tok_dev)
    meta = meta.transpose(2, 1, 3, 0, 4).reshape(2, sources, top, group)

    both = jnp.stack([inputs, out_grad])
    both = lax.all_to_all(both, "rep", split_axis=2, concat_axis=1, tiled=True)
    both = lax.all_gather(both, "exp", axis=0, tiled=False)

    first = lax.axis_index("exp") * local
    mine = (first + jnp.arange(local, dtype=jnp.int32)).astype(F32)
    hit = meta[0][:, None] == mine[None, :, None, None]
    named = jnp.any(hit, axis=2)
    gate = jnp.sum(jnp.where(hit, meta[1][:, None], 0.0), axis=2)
    earlier = jnp.arange(group)[:, None] < jnp.arange(group)[None, :]
    rank = jnp.einsum(
        "glt,tu->glu", named.astype(BF16), earlier.astype(BF16), preferred_element_type=F32
    )
    rank = jnp.where(named, rank, -1.0)
    onehot = rank[:, :, None, :] == jnp.arange(slots, dtype=F32)[None, None, :, None]
    gate_slot = jnp.sum(jnp.where(onehot, gate[:, :, None, :], 0.0), axis=3)
    pick = onehot.astype(BF16)

    me = lax.axis_index("rep")
    per = sources // replicas

    def own(array, q):
        return lax.dynamic_slice_in_dim(array, (me ^ q) * per, per, 0)

    def swap(array, bit):
        return lax.ppermute(array, "rep", [(i, i ^ bit) for i in range(replicas)])

    mats = weights.transpose(1, 0, 2, 3).reshape(local, part, kinds * ffn)
    pair_mats, down_mats = mats[..., :pair], mats[..., pair:]
    picks = [own(pick, q) for q in range(replicas)]
    rows_x, rows_g, sums = {}, {}, {}
    for q in reversed(range(replicas)):
        tokens = own(both, q)
        x = jnp.einsum("glst,gtd->glsd", picks[q], tokens[:, 0], preferred_element_type=F32)
        g = jnp.einsum("glst,gtd->glsd", picks[q], tokens[:, 1], preferred_element_type=F32)
        g = g * own(gate_slot, q)[..., None]
        rows_x[q] = x.astype(BF16).transpose(1, 0, 2, 3).reshape(local, per * slots, part)
        rows_g[q] = g.astype(BF16).transpose(1, 0, 2, 3).reshape(local, per * slots, part)
        hidden = jnp.einsum("lrd,ldh->lrh", rows_x[q], pair_mats, preferred_element_type=F32)
        da = jnp.einsum("lrd,ldh->lrh", rows_g[q], down_mats, preferred_element_type=F32)
        sums[q] = (hidden, da)

    bit, live = 1, list(range(replicas))
    while bit < replicas:
        for q in reversed([q for q in live if q & bit]):
            sums[q ^ bit] = tuple(
                mine + swap(theirs.astype(BF16), bit).astype(F32)
                for mine, theirs in zip(sums[q ^ bit], sums[q])
            )
        live = [q for q in live if not q & bit]
        bit *= 2
    hidden, da = sums[0]
    hg, hu = hidden[..., :ffn], hidden[..., ffn:]
    sig = jax.nn.sigmoid(hg)
    act = (hg * sig * hu).astype(BF16)
    dhu = (da * hg * sig).astype(BF16)
    dhg = (da * hu * sig * (1.0 + hg * (1.0 - sig))).astype(BF16)
    d_pair, acts = {0: jnp.concatenate([dhg, dhu], axis=2)}, {0: act}
    for held in (d_pair, acts):
        bit = replicas // 2
        while bit:
            for q in list(held):
                held[q ^ bit] = swap(held[q], bit)
            bit //= 2

    token_dx = []
    for q in range(replicas):
        slot_dx = jnp.einsum(
            "lrh,ldh->lrd", d_pair[q], pair_mats, preferred_element_type=F32
        ).astype(BF16)
        slot_dx = slot_dx.reshape(local, per, slots, part)
        dx = jnp.einsum("glst,lgsd->gtd", picks[q], slot_dx, preferred_element_type=F32)
        token_dx.append(dx.astype(BF16))
    token_dx = jnp.stack(token_dx)
    token_dx = jnp.concatenate(
        [lax.dynamic_index_in_dim(token_dx, me ^ q, 0, keepdims=False) for q in range(replicas)]
    )
    token_dx = lax.psum_scatter(token_dx, "exp", scatter_dimension=0, tiled=False)
    input_grad = lax.all_to_all(token_dx, "rep", split_axis=0, concat_axis=1, tiled=True)

    def whole(pieces):
        return jnp.concatenate([pieces[q] for q in range(replicas)], axis=1)

    rows_x, rows_g, d_pair, acts = whole(rows_x), whole(rows_g), whole(d_pair), whole(acts)
    grads = []
    for kind in range(kinds):
        left = rows_x if kind < 2 else rows_g
        right = d_pair[..., kind * ffn : (kind + 1) * ffn] if kind < 2 else acts
        one = jnp.einsum("lrd,lrh->ldh", left, right, preferred_element_type=F32)
        grads.append(with_layout_constraint(one.transpose(1, 0, 2), Layout((0, 1, 2))))
    grad = with_layout_constraint(jnp.stack(grads, axis=2), Layout((0, 2, 1, 3)))

    first_moment = beta_one * moment_one + (1.0 - beta_one) * grad
    second_moment = beta_two * moment_two + (1.0 - beta_two) * grad * grad
    correct_one = 1.0 - beta_one**step_count
    correct_two = 1.0 - beta_two**step_count
    weights32 = weights.astype(F32)
    update = (
        first_moment / correct_one / (jnp.sqrt(second_moment / correct_two) + epsilon)
        + decay_rate * weights32
    )
    new_weights = (weights32 - learn_rate * update).astype(BF16)
    return (input_grad, first_moment, second_moment, new_weights)


def solution(mesh):
    tokens = P(("rep", "exp"), None)
    experts = P("rep", "exp", None, None)
    return jax.shard_map(
        per_device,
        mesh=mesh,
        in_specs=(tokens, tokens, tokens, tokens, experts, experts, experts),
        out_specs=(tokens, experts, experts, experts),
        check_vma=False,
    )
```

```python
import jax
import jax.numpy as jnp
from jax import lax
from jax.experimental.layout import Layout, with_layout_constraint
from jax.sharding import PartitionSpec as P


CAP = 18


beta_one = 0.9
beta_two = 0.95
learn_rate = 0.002
decay_rate = 0.1
epsilon = 1e-08
step_count = 100

F32 = jnp.float32
BF16 = jnp.bfloat16


def per_device(inputs, out_grad, routes, gates, weights, moment_one, moment_two):
    replicas, sources = lax.axis_size("rep"), lax.axis_size("exp")
    tok_dev, top = routes.shape
    part, local, kinds, ffn = weights.shape
    pair = 2 * ffn
    slots = sources * CAP
    me = lax.axis_index("rep")

    def swap(array, bits):
        if bits == 0:
            return array
        return lax.ppermute(array, "rep", [(i, i ^ bits) for i in range(replicas)])

    terms, rest = [routes.astype(BF16).T], gates.T
    for _ in range(3):
        head = lax.reduce_precision(rest, 8, 7)
        terms.append(head.astype(BF16))
        rest = rest - head
    meta = jnp.concatenate(terms).reshape(-1, part)
    meta_rows = meta.shape[0]
    pad = -meta_rows % 16
    meta = jnp.pad(meta, ((0, pad), (0, 0)))

    def arrive(q):
        at = (me ^ q) * part
        x = lax.dynamic_slice_in_dim(inputs, at, part, 1)
        g = lax.dynamic_slice_in_dim(out_grad, at, part, 1)
        return swap(jnp.concatenate([x, g, meta]), q)

    gathered = {}
    half = max(replicas // 2, 1)
    for start in range(replicas - half, -1, -half):
        chosen = range(start, start + half)
        block = jnp.stack([arrive(q) for q in reversed(chosen)])
        block = lax.all_gather(block, "exp", axis=0, tiled=False)
        for place, q in enumerate(reversed(chosen)):
            gathered[q] = block[:, place]

    mine = lax.axis_index("exp") * local + jnp.arange(local, dtype=jnp.int32)
    earlier = jnp.arange(tok_dev)[:, None] < jnp.arange(tok_dev)[None, :]
    base = (jnp.arange(sources) * CAP).astype(F32)
    mats = weights.transpose(1, 0, 2, 3).reshape(local, part, kinds * ffn)
    pair_mats, down_mats = mats[..., :pair], mats[..., pair:]
    picks, rows_x, rows_g, arrivals = {}, {}, {}, {}
    for q in reversed(range(replicas)):
        if q == half - 1 and replicas > 1:
            later = {p: gathered[p] for p in range(half)}
            later, _ = lax.optimization_barrier((later, sent))
            gathered.update(later)
        got = gathered[q]
        info = got[:, 2 * tok_dev : 2 * tok_dev + meta_rows].astype(F32)
        info = info.reshape(sources, 4, top, tok_dev)
        weight = info[:, 1] + info[:, 2] + info[:, 3]
        hit = info[:, 0][None] == mine.astype(F32)[:, None, None, None]
        named = jnp.any(hit, axis=2)
        gate = jnp.sum(jnp.where(hit, weight[None], 0.0), axis=2)
        rank = jnp.einsum(
            "let,tu->leu", named.astype(BF16), earlier.astype(BF16), preferred_element_type=F32
        )
        rank = jnp.where(named, rank + base[None, :, None], -1.0)
        rank = rank.reshape(local, 1, sources * tok_dev)
        onehot = rank == jnp.arange(slots, dtype=F32)[None, :, None]
        gate = gate.reshape(local, 1, sources * tok_dev)
        gate_slot = jnp.sum(jnp.where(onehot, gate, 0.0), axis=2)
        picks[q] = onehot.astype(BF16)
        tokens_x = got[:, :tok_dev].reshape(sources * tok_dev, part)
        tokens_g = got[:, tok_dev : 2 * tok_dev].reshape(sources * tok_dev, part)
        x = jnp.einsum("lst,td->lsd", picks[q], tokens_x, preferred_element_type=F32)
        g = jnp.einsum("lst,td->lsd", picks[q], tokens_g, preferred_element_type=F32)
        rows_x[q] = x.astype(BF16)
        rows_g[q] = (g * gate_slot[..., None]).astype(BF16)
        hidden = jnp.einsum("lrd,ldh->lrh", rows_x[q], pair_mats, preferred_element_type=F32)
        da = jnp.einsum("lrd,ldh->lrh", rows_g[q], down_mats, preferred_element_type=F32)
        sums = [hidden, da]
        for term in arrivals.pop(q, []):
            sums = [old + new.astype(F32) for old, new in zip(sums, term)]
        sent = [one.astype(BF16) for one in sums]
        if q:
            arrivals.setdefault(q & (q - 1), []).append([swap(one, q & -q) for one in sent])

    hidden, da = sums
    hg, hu = hidden[..., :ffn], hidden[..., ffn:]
    sig = jax.nn.sigmoid(hg)
    act = (hg * sig * hu).astype(BF16)
    dhu = (da * hg * sig).astype(BF16)
    dhg = (da * hu * sig * (1.0 + hg * (1.0 - sig))).astype(BF16)
    d_pair, acts = {0: jnp.concatenate([dhg, dhu], axis=2)}, {0: act}
    for held in (d_pair, acts):
        bit = replicas // 2
        while bit:
            for q in list(held):
                held[q ^ bit] = swap(held[q], bit)
            bit //= 2

    token_dx = {}
    for q in range(replicas):
        slot_dx = jnp.einsum(
            "lrh,ldh->lrd", d_pair[q], pair_mats, preferred_element_type=F32
        ).astype(BF16)
        dx = jnp.einsum("lst,lsd->td", picks[q], slot_dx, preferred_element_type=F32)
        token_dx[q] = dx.astype(BF16).reshape(sources, tok_dev, part)
    home = {}
    for start in range(0, replicas, half):
        block = jnp.concatenate([token_dx[q] for q in range(start, start + half)], axis=1)
        block = lax.psum_scatter(block, "exp", scatter_dimension=0, tiled=False)
        for place in range(half):
            one = block[place * tok_dev : (place + 1) * tok_dev]
            home[start + place] = swap(one, start + place)
    home = jnp.stack([home[q] for q in range(replicas)])
    input_grad = jnp.concatenate(
        [lax.dynamic_index_in_dim(home, me ^ q, 0, keepdims=False) for q in range(replicas)],
        axis=1,
    )

    def whole(pieces):
        return jnp.concatenate([pieces[q] for q in range(replicas)], axis=1)

    rows_x, rows_g, d_pair, acts = whole(rows_x), whole(rows_g), whole(d_pair), whole(acts)
    grads = []
    for kind in range(kinds):
        left = rows_x if kind < 2 else rows_g
        right = d_pair[..., kind * ffn : (kind + 1) * ffn] if kind < 2 else acts
        one = jnp.einsum("lrd,lrh->ldh", left, right, preferred_element_type=F32)
        grads.append(with_layout_constraint(one.transpose(1, 0, 2), Layout((0, 1, 2))))
    grad = with_layout_constraint(jnp.stack(grads, axis=2), Layout((0, 2, 1, 3)))

    first_moment = beta_one * moment_one + (1.0 - beta_one) * grad
    second_moment = beta_two * moment_two + (1.0 - beta_two) * grad * grad
    correct_one = 1.0 - beta_one**step_count
    correct_two = 1.0 - beta_two**step_count
    weights32 = weights.astype(F32)
    update = (
        first_moment / correct_one / (jnp.sqrt(second_moment / correct_two) + epsilon)
        + decay_rate * weights32
    )
    new_weights = (weights32 - learn_rate * update).astype(BF16)
    return (input_grad, first_moment, second_moment, new_weights)


def solution(mesh):
    tokens = P(("rep", "exp"), None)
    experts = P("rep", "exp", None, None)
    return jax.shard_map(
        per_device,
        mesh=mesh,
        in_specs=(tokens, tokens, tokens, tokens, experts, experts, experts),
        out_specs=(tokens, experts, experts, experts),
        check_vma=False,
    )
```
